32 devices in a mesh: gx: 4 (over y, x), gy: 8 (over z, core).
Axes of the slice: x: 2, y: 2, z: 4, core: 2. Of those that a mesh axis runs over, the one named last changes fastest.
Arguments:
- cam_pose: float32 [7, 8192], P(None, ('gx', 'gy')), may hold values from -0.5 to 2, as said below
- points: float32 [3, 131072], P(None, ('gx', 'gy')), may hold values from -1.5 to 8, as said below
- obs_uv: float32 [2, 32, 32, 128], P(None, ('gx', 'gy')), may hold values from -0.6 to 0.6
- obs_cam: int32 [32, 32, 128], P(('gx', 'gy')), may hold values from 0 to 255
- obs_pt: int32 [32, 32, 128], P(('gx', 'gy')), may hold values from 0 to 4095
- block_count: int32 [32, 32], P(('gx', 'gy')), may hold values from 1 to 128, as said below
- send_list: int32 [32, 32, 16], P(('gx', 'gy')), may hold values from 0 to 255
- edge_slot: int32 [8, 8192], P(None, ('gx', 'gy')), may hold values from 0 to 511
- edge_weight: float32 [8, 8192], P(None, ('gx', 'gy')), may hold values from 0.2 to 1
Outputs:
- cam_step: float32 [6, 8192], P(None, ('gx', 'gy'))
- cam_residual: float32 [6, 8192], P(None, ('gx', 'gy'))
The draws below stay inside these ranges and needn't reach their ends.
Inputs may be any that keep to these rules, and one draw needn't show every extreme that they name: `cam_pose`: rows 0 in [0.9, 1.1], rows 1 to 3 in [-0.15, 0.15], rows 4 and 5 in [-0.5, 0.5], row 6 in [1, 2]. `points`: rows 0 and 1 in [-1.5, 1.5], row 2 in [4, 8]. Slot j of block [d, s] is live exactly when j < block_count[d, s]; some blocks are full.
All inputs are finite; a program needn't handle non-finite values.
Results may differ from the reference program's by a relative error of at most 0.00021.
Values sent between devices are 32-bit elements; how exact they have to be, the bound alone decides.
A program may use at most 64 MiB of HBM per device.

```python
import math
import jax
import jax.numpy as jnp

SLOT = 128
CSLOT = 16
NEIGHBORS = 8
ITERS = 2
CAM_DEV = 256
PT_DEV = 4096
CAMS = 8192
PTS = 131072
N_GX = 4
N_GY = 8


def draw_cam_pose(key, part):
    keys = jax.random.split(key, 4)
    lead = jax.random.uniform(keys[0], (1, CAMS), jnp.float32, 0.9, 1.1)
    vector_part = jax.random.uniform(keys[1], (3, CAMS), jnp.float32, -0.15, 0.15)
    shift = jax.random.uniform(keys[2], (2, CAMS), jnp.float32, -0.5, 0.5)
    height = jax.random.uniform(keys[3], (1, CAMS), jnp.float32, 1.0, 2.0)
    return jnp.concatenate([lead, vector_part, shift, height], 0)


def draw_points(key, part):
    keys = jax.random.split(key, 2)
    planar = jax.random.uniform(keys[0], (2, PTS), jnp.float32, -1.5, 1.5)
    height = jax.random.uniform(keys[1], (1, PTS), jnp.float32, 4.0, 8.0)
    return jnp.concatenate([planar, height], 0)


def draw_block_count(key, part):
    devices = N_GX * N_GY
    keys = jax.random.split(key, 4)
    heavy = jax.random.randint(keys[0], (devices,), 0, 8) == 0
    forced = jax.random.randint(keys[1], (), 0, devices)
    heavy = heavy | (jnp.arange(devices) == forced)
    lowest = max(SLOT // 4, 1)
    capacity = jnp.where(heavy, SLOT, max(2 * SLOT // 3, lowest)).astype(jnp.int32)
    counts = jax.random.randint(keys[2], (devices, devices), lowest, capacity[:, None] + 1)
    full_source = jax.random.randint(keys[3], (devices,), 0, devices)
    filled = heavy[:, None] & (jnp.arange(devices)[None, :] == full_source[:, None])
    return jnp.where(filled, SLOT, counts).astype(jnp.int32)


def set_ends(array, rng, low, largest):
    spot = [jax.random.randint(jax.random.fold_in(rng, axis), (), 0, length) for axis, length in enumerate(array.shape)]
    widest = array.shape.index(max(array.shape))
    beside = spot[:widest] + [(spot[widest] + 1) % array.shape[widest]] + spot[widest + 1:]
    return array.at[tuple(spot)].set(low).at[tuple(beside)].set(largest)


def block_levels(rng, shape, cuts, smallest, largest):
    loudness, own = 1.0, jax.random.fold_in(rng, 6)
    for dim, parts in cuts:
        steps = jnp.exp(jax.random.uniform(jax.random.fold_in(own, dim), (parts,), jnp.float32, smallest / len(cuts), largest / len(cuts)))
        loudness = loudness * jnp.repeat(steps, shape[dim] // parts).reshape([-1 if axis == dim else 1 for axis in range(len(shape))])
    return loudness


def setup_inputs(seed: int = 0) -> dict:
    key_of = jax.random.split(jax.random.key(seed), 10)
    return {
        "cam_pose": draw_cam_pose(jax.random.fold_in(key_of[9], 71), 0),
        "points": draw_points(jax.random.fold_in(key_of[9], 71), 0),
        "obs_uv": jnp.clip(jax.random.uniform(key_of[2], (2, N_GX * N_GY, N_GX * N_GY, SLOT), jnp.float32, -0.6, 0.6) * block_levels(key_of[2], (2, N_GX * N_GY, N_GX * N_GY, SLOT), ((1, 32),), -0.4, 0.0), -0.6, 0.6),
        "obs_cam": set_ends(jax.random.randint(key_of[3], (N_GX * N_GY, N_GX * N_GY, SLOT), 0, CAM_DEV), jax.random.fold_in(key_of[3], 1), 0, CAM_DEV - 1).astype(jnp.int32),
        "obs_pt": set_ends(jax.random.randint(key_of[4], (N_GX * N_GY, N_GX * N_GY, SLOT), 0, PT_DEV), jax.random.fold_in(key_of[4], 1), 0, PT_DEV - 1).astype(jnp.int32),
        "block_count": draw_block_count(jax.random.fold_in(key_of[9], 71), 0),
        "send_list": set_ends(jax.random.randint(key_of[6], (N_GX * N_GY, N_GX * N_GY, CSLOT), 0, CAM_DEV), jax.random.fold_in(key_of[6], 1), 0, CAM_DEV - 1).astype(jnp.int32),
        "edge_slot": set_ends(jax.random.randint(key_of[7], (NEIGHBORS, CAMS), 0, N_GX * N_GY * CSLOT), jax.random.fold_in(key_of[7], 1), 0, (N_GX * N_GY * CSLOT) - 1).astype(jnp.int32),
        "edge_weight": jnp.clip(jnp.exp(math.log(1.0) - 1.609438 * jax.random.uniform(key_of[8], (NEIGHBORS, CAMS), jnp.float32) ** block_levels(key_of[8], (NEIGHBORS, CAMS), ((1, 32),), -0.2, 0.2)), 0.2, 1.0),
    }


DAMPING = 1.0
SYMMETRIC_PAIRS = [(a, b) for a in range(6) for b in range(a, 6)]
POINT_PAIRS = [(0, 0), (0, 1), (0, 2), (1, 1), (1, 2), (2, 2)]


def rotation(quaternion):
    q0, q1, q2, q3 = quaternion[0], quaternion[1], quaternion[2], quaternion[3]
    inverse_norm = 1.0 / (q0 * q0 + q1 * q1 + q2 * q2 + q3 * q3)
    entries = [q0 * q0 + q1 * q1 - q2 * q2 - q3 * q3, 2.0 * (q1 * q2 - q0 * q3), 2.0 * (q1 * q3 + q0 * q2),
               2.0 * (q1 * q2 + q0 * q3), q0 * q0 - q1 * q1 + q2 * q2 - q3 * q3, 2.0 * (q2 * q3 - q0 * q1),
               2.0 * (q1 * q3 - q0 * q2), 2.0 * (q2 * q3 + q0 * q1), q0 * q0 - q1 * q1 - q2 * q2 + q3 * q3]
    return jnp.stack([value * inverse_norm for value in entries])


def eliminate(measured, rot_rows, translation, point_rows, live_mask, point_index, count_points):
    cam_pt = [rot_rows[3 * a] * point_rows[0] + rot_rows[3 * a + 1] * point_rows[1] + rot_rows[3 * a + 2] * point_rows[2] + translation[a] for a in range(3)]
    inv_depth = 1.0 / cam_pt[2]
    proj_u = cam_pt[0] * inv_depth
    proj_v = cam_pt[1] * inv_depth
    residue = [(proj_u - measured[0]) * live_mask, (proj_v - measured[1]) * live_mask]
    scaled = inv_depth * live_mask
    zeros_row = jnp.zeros_like(scaled)
    jac_proj = [[scaled, zeros_row, -proj_u * scaled], [zeros_row, scaled, -proj_v * scaled]]
    cross_matrix = [[zeros_row, cam_pt[2], -cam_pt[1]], [-cam_pt[2], zeros_row, cam_pt[0]], [cam_pt[1], -cam_pt[0], zeros_row]]
    jac_cam = []
    jac_point = []
    for i in range(2):
        jac_row = [jac_proj[i][0] * cross_matrix[0][k] + jac_proj[i][1] * cross_matrix[1][k] + jac_proj[i][2] * cross_matrix[2][k] for k in range(3)]
        jac_cam.append(jac_row + jac_proj[i])
        jac_point.append([jac_proj[i][0] * rot_rows[k] + jac_proj[i][1] * rot_rows[3 + k] + jac_proj[i][2] * rot_rows[6 + k] for k in range(3)])
    point_terms = [jac_point[0][k] * jac_point[0][l] + jac_point[1][k] * jac_point[1][l] for (k, l) in POINT_PAIRS]
    point_terms = point_terms + [jac_point[0][k] * residue[0] + jac_point[1][k] * residue[1] for k in range(3)]
    point_sums = jnp.zeros((9, count_points), jnp.float32).at[:, point_index].add(jnp.stack(point_terms))
    hess = [point_sums[0] + DAMPING, point_sums[1], point_sums[2], point_sums[3] + DAMPING, point_sums[4], point_sums[5] + DAMPING]
    cofactor = [hess[3] * hess[5] - hess[4] * hess[4], hess[2] * hess[4] - hess[1] * hess[5], hess[1] * hess[4] - hess[2] * hess[3],
                hess[0] * hess[5] - hess[2] * hess[2], hess[1] * hess[2] - hess[0] * hess[4], hess[0] * hess[3] - hess[1] * hess[1]]
    determinant = hess[0] * cofactor[0] + hess[1] * cofactor[1] + hess[2] * cofactor[2]
    per_point = jnp.stack([value / determinant for value in cofactor] + [point_sums[6], point_sums[7], point_sums[8]])[:, point_index]
    inv_full = [[per_point[0], per_point[1], per_point[2]], [per_point[1], per_point[3], per_point[4]], [per_point[2], per_point[4], per_point[5]]]
    grad_point = [per_point[6], per_point[7], per_point[8]]
    coupling = [[jac_cam[0][a] * jac_point[0][k] + jac_cam[1][a] * jac_point[1][k] for k in range(3)] for a in range(6)]
    coupled = [[coupling[a][0] * inv_full[0][k] + coupling[a][1] * inv_full[1][k] + coupling[a][2] * inv_full[2][k] for k in range(3)] for a in range(6)]
    schur_block = [jac_cam[0][a] * jac_cam[0][b] + jac_cam[1][a] * jac_cam[1][b] - (coupled[a][0] * coupling[b][0] + coupled[a][1] * coupling[b][1] + coupled[a][2] * coupling[b][2]) for (a, b) in SYMMETRIC_PAIRS]
    reduced = [jac_cam[0][a] * residue[0] + jac_cam[1][a] * residue[1] - (coupled[a][0] * grad_point[0] + coupled[a][1] * grad_point[1] + coupled[a][2] * grad_point[2]) for a in range(6)]
    return jnp.stack(schur_block + reduced)


def block_product(blocks, vector):
    lookup = {}
    for index, (a, b) in enumerate(SYMMETRIC_PAIRS):
        lookup[(a, b)] = index
        lookup[(b, a)] = index
    return jnp.stack([sum(blocks[lookup[(a, b)]] * vector[b] for b in range(6)) for a in range(6)])


def reference(cam_pose, points, obs_uv, obs_cam, obs_pt, block_count, send_list, edge_slot, edge_weight):
    devices = N_GX * N_GY
    shape = (devices, devices, SLOT)
    source = jax.lax.broadcasted_iota(jnp.int32, shape, 0)
    target = jax.lax.broadcasted_iota(jnp.int32, shape, 1)
    position = jax.lax.broadcasted_iota(jnp.int32, shape, 2)
    cam_global = (source * CAM_DEV + obs_cam).reshape(-1)
    pt_global = (target * PT_DEV + jnp.transpose(obs_pt, (1, 0, 2))).reshape(-1)
    live_mask = (position < jnp.transpose(block_count)[:, :, None]).astype(jnp.float32).reshape(-1)
    rot_rows = rotation(cam_pose[0:4])[:, cam_global]
    translation = cam_pose[4:7][:, cam_global]
    measured = obs_uv.reshape(2, -1)
    entries = eliminate(measured, rot_rows, translation, points[:, pt_global], live_mask, pt_global, PTS)
    camera_sums = jnp.zeros((27, CAMS), jnp.float32).at[:, cam_global].add(entries)
    blocks = camera_sums[0:21]
    gradient = camera_sums[21:27]
    owner_device = (jnp.arange(CAMS) // CAM_DEV).astype(jnp.int32)
    from_device = (edge_slot // CSLOT).astype(jnp.int32)
    neighbour = from_device * CAM_DEV + send_list[from_device, owner_device[None, :], edge_slot % CSLOT]
    flat_neighbour = neighbour.reshape(-1)

    def apply_system(vector):
        edge_term = edge_weight[None] * (vector[:, None, :] - vector[:, neighbour])
        applied = block_product(blocks, vector) + DAMPING * vector + jnp.sum(edge_term, axis=1)
        return applied.at[:, flat_neighbour].add(-edge_term.reshape(6, -1))

    diagonal_entries = jnp.stack([blocks[SYMMETRIC_PAIRS.index((a, a))] for a in range(6)]) + DAMPING
    update_step = jnp.zeros((6, CAMS), jnp.float32)
    residual = -gradient
    precond = residual / diagonal_entries
    direction = precond
    precond_dot = jnp.sum(residual * precond)
    for iteration in range(ITERS):
        product_image = apply_system(direction)
        step_size = precond_dot / jnp.sum(direction * product_image)
        update_step = update_step + step_size * direction
        residual = residual - step_size * product_image
        if iteration + 1 < ITERS:
            precond = residual / diagonal_entries
            next_dot = jnp.sum(residual * precond)
            direction = precond + (next_dot / precond_dot) * direction
            precond_dot = next_dot
    return update_step, residual
```

```python
import functools
import math

import jax
import jax.numpy as jnp
from jax import lax
from jax.experimental import pallas as pl
from jax.experimental.pallas import tpu as pltpu
from jax.sharding import PartitionSpec as P

ITERS = 2
DAMPING = 1.0
LANES = 128
MESH = pl.DeviceIdType.MESH
PAIRS = [(a, b) for a in range(6) for b in range(a, 6)]
F32 = jnp.float32
BF16 = jnp.bfloat16


def iota(shape, axis):
    return lax.broadcasted_iota(jnp.int32, shape, axis)


def head(x):
    return x.astype(BF16).astype(F32)


def split2(x):
    high = head(x)
    return jnp.concatenate([high, x - high], 0).astype(BF16)


def split3(x):
    high = head(x)
    rest = x - high
    middle = head(rest)
    return jnp.concatenate([high, middle, rest - middle], 0).astype(BF16)


def dot(a, b):
    return jnp.dot(a, b, preferred_element_type=F32)


def dot_nt(a, b):
    return lax.dot_general(a, b, (((1,), (1,)), ((), ())), preferred_element_type=F32)


def block_transpose(x):
    off = jnp.bitwise_and((iota((8, LANES), 1) >> 4) - iota((8, LANES), 0), 7)
    out = x
    for s in range(1, 8):
        moved = pltpu.roll(pltpu.roll(x, 8 - s, 0), 16 * s, 1)
        out = jnp.where(off == s, moved, out)
    return out


def to_rows(x):
    tiles = x.shape[1] // LANES
    return jnp.concatenate(
        [block_transpose(x[:, t * LANES : (t + 1) * LANES]) for t in range(tiles)], 0
    )


def to_columns(x):
    tiles = x.shape[0] // 8
    return jnp.concatenate([block_transpose(x[8 * t : 8 * t + 8]) for t in range(tiles)], 1)


def kernel(
    nx,
    ny,
    cam_ref,
    pts_ref,
    uv_ref,
    oc_ref,
    op_ref,
    cnt_ref,
    snd_ref,
    es_ref,
    ew_ref,
    step_ref,
    res_ref,
    tx1,
    rx1,
    tx2,
    rx2,
    txc,
    rxc,
    ohp,
    ohc,
    xbuf,
    vbuf,
    acc0,
    acc1,
    tab0,
    tab1,
    gbuf,
    cbuf,
    cacc,
    s_hi,
    s_lo,
    send_sem,
    recv_sem,
):
    devices = nx * ny
    cams = cam_ref.shape[1]
    width = math.gcd(pts_ref.shape[1], 2 * LANES)
    levels = pts_ref.shape[1] // width
    group = math.gcd(devices, 4)
    span = group * LANES
    me = lax.axis_index("gx") * ny + lax.axis_index("gy")

    barrier = pltpu.get_barrier_semaphore()

    def greet(i, c):
        peer = lax.rem(me + i, devices)
        pl.semaphore_signal(
            barrier, inc=1, device_id=(peer // ny, lax.rem(peer, ny)), device_id_type=MESH
        )
        return c

    lax.fori_loop(1, devices, greet, 0)

    def send(rnd, tx, rx, rows):
        def one(i, c):
            peer = lax.rem(me + i, devices)
            pltpu.make_async_remote_copy(
                src_ref=tx.at[pl.ds(peer * rows, rows)],
                dst_ref=rx.at[pl.ds(me * rows, rows)],
                send_sem=send_sem.at[rnd],
                recv_sem=recv_sem.at[rnd],
                device_id=(peer // ny, lax.rem(peer, ny)),
                device_id_type=MESH,
            ).start()
            return c

        lax.fori_loop(1, devices, one, 0)
        rx[pl.ds(me * rows, rows)] = tx[pl.ds(me * rows, rows)]

    def wait(rnd, ref, rows, sem):
        part = ref.at[pl.ds(0, (devices - 1) * rows)]
        pltpu.make_async_copy(part, part, sem.at[rnd]).wait()

    pose = cam_ref[...]
    table = split3(
        jnp.concatenate([jnp.zeros((2, cams), F32), pose[1:4] / pose[0:1], pose[4:7]], 0)
    )
    row8 = iota((8, LANES), 0)

    def gather_poses(i, c):
        rows = [oc_ref[0, pl.ds(i * group + g, 1), :] for g in range(group)]
        onehot = (iota((cams, span), 0) == jnp.concatenate(rows, 1)).astype(F32).astype(BF16)
        ohc[:, pl.ds(pl.multiple_of(i * span, span), span)] = onehot
        got = dot(table, onehot)
        got = got[0:8] + got[8:16] + got[16:24]
        for g in range(group):
            d = i * group + g
            block = got[:, g * LANES : (g + 1) * LANES]
            block = jnp.where(row8 == 0, uv_ref[0, 0, pl.ds(d, 1), :], block)
            block = jnp.where(row8 == 1, uv_ref[1, 0, pl.ds(d, 1), :], block)
            tx1[pl.ds(pl.multiple_of(d * 8, 8), 8), :] = block
        return c

    lax.fori_loop(0, devices // group, gather_poses, 0)
    pl.semaphore_wait(barrier, devices - 1)
    send(0, tx1, rx1, 8)

    def level_mask(i):
        rows = [op_ref[0, pl.ds(i * group + g, 1), :] for g in range(group)]
        row = jnp.concatenate(rows, 1)
        level = row // width
        return row - level * width, (iota((levels, span), 0) == level).astype(F32)

    positions = jnp.concatenate([pts_ref[...], jnp.zeros((5, levels * width), F32)], 0)
    positions = split3(
        jnp.concatenate([positions[:, k * width : (k + 1) * width] for k in range(levels)], 0)
    )
    part = levels * 8

    def gather_tracks(i, c):
        low, mask = level_mask(i)
        onehot = (iota((width, span), 0) == low).astype(F32).astype(BF16)
        ohp[:, pl.ds(pl.multiple_of(i * span, span), span)] = onehot
        got = dot(positions, onehot)
        got = got[0:part] + got[part : 2 * part] + got[2 * part : 3 * part]
        total = jnp.zeros((8, span), F32)
        for k in range(levels):
            total = total + got[k * 8 : k * 8 + 8] * mask[k : k + 1]
        for g in range(group):
            d = i * group + g
            xbuf[pl.ds(pl.multiple_of(d * 8, 8), 8), :] = total[:, g * LANES : (g + 1) * LANES]
        return c

    lax.fori_loop(0, devices // group, gather_tracks, 0)

    slots = snd_ref.shape[1]
    piece = 64

    def weigh(i, c):
        slot = iota((piece, cams), 0) + i * piece
        total = jnp.zeros((piece, cams), F32)
        for k in range(es_ref.shape[0]):
            total = total + jnp.where(slot == es_ref[k : k + 1, :], ew_ref[k : k + 1, :], 0.0)
        high = head(total)
        at = pl.ds(pl.multiple_of(i * piece, piece), piece)
        s_hi[at, :] = high.astype(BF16)
        s_lo[at, :] = (total - high).astype(BF16)
        return c

    lax.fori_loop(0, slots // piece, weigh, 0)
    ohs = (iota((cams, slots), 0) == snd_ref[...]).astype(F32).astype(BF16)
    degree = jnp.sum(ew_ref[...], 0, keepdims=True)
    ones = jnp.ones((16, cams), F32).astype(BF16)
    slot_degree = (dot_nt(ones, s_hi[...]) + dot_nt(ones, s_lo[...]))[0:1]

    spread = jnp.where(
        iota((devices, devices), 0) == iota((devices, devices), 1), cnt_ref[...].astype(F32), 0.0
    )
    count = jnp.sum(spread, 1, keepdims=True)
    live = (iota((devices, LANES), 1).astype(F32) < count).astype(F32)

    vbuf[...] = jnp.zeros_like(vbuf)
    acc0[...] = jnp.zeros_like(acc0)
    acc1[...] = jnp.zeros_like(acc1)
    tab0[...] = jnp.zeros_like(tab0)
    tab1[...] = jnp.zeros_like(tab1)
    cbuf[...] = jnp.zeros_like(cbuf)
    cacc[...] = jnp.zeros_like(cacc)

    wait(0, rx1, 8, recv_sem)

    def pick(ref, r, stride):
        return ref[pl.ds(r, devices, stride=stride), :]

    mu, mv, q1, q2, q3, t0, t1, t2 = [pick(rx1, r, 8) for r in range(8)]
    x0, x1, x2 = [pick(xbuf, r, 8) for r in range(3)]
    norm = 1.0 / (1.0 + q1 * q1 + q2 * q2 + q3 * q3)
    rot = [
        1.0 + q1 * q1 - q2 * q2 - q3 * q3,
        2.0 * (q1 * q2 - q3),
        2.0 * (q1 * q3 + q2),
        2.0 * (q1 * q2 + q3),
        1.0 - q1 * q1 + q2 * q2 - q3 * q3,
        2.0 * (q2 * q3 - q1),
        2.0 * (q1 * q3 - q2),
        2.0 * (q2 * q3 + q1),
        1.0 - q1 * q1 - q2 * q2 + q3 * q3,
    ]
    rot = [r * norm for r in rot]
    pa = rot[0] * x0 + rot[1] * x1 + rot[2] * x2 + t0
    pb = rot[3] * x0 + rot[4] * x1 + rot[5] * x2 + t1
    pe = rot[6] * x0 + rot[7] * x1 + rot[8] * x2 + t2
    inv = 1.0 / pe
    u = pa * inv
    v = pb * inv
    scaled = inv * live
    ru = (u - mu) * live
    rv = (v - mv) * live
    ju = [scaled * (rot[k] - u * rot[6 + k]) for k in range(3)]
    jv = [scaled * (rot[3 + k] - v * rot[6 + k]) for k in range(3)]
    terms = [ju[k] * ju[l] + jv[k] * jv[l] for k in range(3) for l in range(k, 3)]
    terms = terms + [ju[k] * ru + jv[k] * rv for k in range(3)]
    for r in range(8):
        vbuf[pl.ds(r, devices, stride=16), :] = terms[r]
    vbuf[pl.ds(8, devices, stride=16), :] = head(terms[8])
    vbuf[pl.ds(9, devices, stride=16), :] = terms[8] - head(terms[8])

    def scatter_tracks(i, c):
        _, mask = level_mask(i)
        blocks = [
            vbuf[pl.ds(pl.multiple_of((i * group + g) * 16, 16), 16), :] for g in range(group)
        ]
        block = jnp.concatenate(blocks, 1)
        high = head(block[0:8])
        rows = jnp.concatenate([high, block[0:8] - high, block[8:16]], 0)
        left = jnp.concatenate([rows * mask[k : k + 1] for k in range(levels)], 0).astype(BF16)
        added = dot_nt(left, ohp[:, pl.ds(pl.multiple_of(i * span, span), span)])
        acc0[...] += added[:, 0:LANES]
        acc1[...] += added[:, LANES:]
        return c

    lax.fori_loop(0, devices // group, scatter_tracks, 0)

    for acc, tab in ((acc0, tab0), (acc1, tab1)):

        def take(r):
            return acc[pl.ds(r, levels, stride=24), :]

        def put(r, value):
            tab[pl.ds(r, levels, stride=24), :] = value

        sums = [take(r) + take(8 + r) for r in range(8)] + [take(16) + take(17)]
        h0, h1, h2, h3, h4, h5 = sums[0:6]
        h0, h3, h5 = h0 + DAMPING, h3 + DAMPING, h5 + DAMPING
        cof = [
            h3 * h5 - h4 * h4,
            h2 * h4 - h1 * h5,
            h1 * h4 - h2 * h3,
            h0 * h5 - h2 * h2,
            h1 * h2 - h0 * h4,
            h0 * h3 - h1 * h1,
        ]
        invdet = 1.0 / (h0 * cof[0] + h1 * cof[1] + h2 * cof[2])
        cof = [value * invdet for value in cof]
        g0, g1, g2 = sums[6:9]
        cof = cof + [
            cof[0] * g0 + cof[1] * g1 + cof[2] * g2,
            cof[1] * g0 + cof[3] * g1 + cof[4] * g2,
            cof[2] * g0 + cof[4] * g1 + cof[5] * g2,
        ]
        for r in range(8):
            put(r, head(cof[r]))
            put(8 + r, cof[r] - head(cof[r]))
        put(16, head(cof[8]))
        put(17, cof[8] - head(cof[8]))

    inverse = jnp.concatenate([tab0[...], tab1[...]], 1).astype(BF16)

    def gather_inverse(i, c):
        _, mask = level_mask(i)
        got = dot(inverse, ohp[:, pl.ds(pl.multiple_of(i * span, span), span)])
        total = jnp.zeros((24, span), F32)
        for k in range(levels):
            total = total + got[k * 24 : k * 24 + 24] * mask[k : k + 1]
        total = jnp.concatenate([total[0:8] + total[8:16], total[16:24]], 0)
        for g in range(group):
            at = pl.ds(pl.multiple_of((i * group + g) * 16, 16), 16)
            gbuf[at, :] = total[:, g * LANES : (g + 1) * LANES]
        return c

    lax.fori_loop(0, devices // group, gather_inverse, 0)

    n = [pick(gbuf, r, 16) for r in range(8)]
    n.append(pick(gbuf, 8, 16) + pick(gbuf, 9, 16))
    full = [[n[0], n[1], n[2]], [n[1], n[3], n[4]], [n[2], n[4], n[5]]]
    nu = [sum(full[k][l] * ju[l] for l in range(3)) for k in range(3)]
    nv = [sum(full[k][l] * jv[l] for l in range(3)) for k in range(3)]
    out = [
        live - sum(ju[k] * nu[k] for k in range(3)),
        -sum(ju[k] * nv[k] for k in range(3)),
        live - sum(jv[k] * nv[k] for k in range(3)),
        ru - sum(ju[k] * n[6 + k] for k in range(3)),
        rv - sum(jv[k] * n[6 + k] for k in range(3)),
        inv,
        u,
        v,
    ]
    for r in range(8):
        tx2[pl.ds(r, devices, stride=8), :] = out[r]
    send(1, tx2, rx2, 8)
    wait(1, rx2, 8, recv_sem)

    muu, muv, mvv, eu, ev, inv, u, v = [pick(rx2, r, 8) for r in range(8)]
    cu = [-u * v, 1.0 + u * u, -v, inv, None, -u * inv]
    cv = [-1.0 - v * v, u * v, u, None, inv, -v * inv]

    def combine(first, second):
        kept = [a * b for a, b in (first, second) if b is not None]
        return kept[0] if len(kept) == 1 else kept[0] + kept[1]

    wu = [combine((muu, cu[a]), (muv, cv[a])) for a in range(6)]
    wv = [combine((muv, cu[a]), (mvv, cv[a])) for a in range(6)]
    for r, (a, b) in enumerate(PAIRS):
        cbuf[pl.ds(r, devices, stride=32), :] = combine((wu[a], cu[b]), (wv[a], cv[b]))
    for a in range(6):
        cbuf[pl.ds(21 + a, devices, stride=32), :] = combine((eu, cu[a]), (ev, cv[a]))

    def scatter_cameras(i, c):
        blocks = [
            cbuf[pl.ds(pl.multiple_of((i * group + g) * 32, 32), 32), :] for g in range(group)
        ]
        left = split2(jnp.concatenate(blocks, 1))
        cacc[...] += dot_nt(left, ohc[:, pl.ds(pl.multiple_of(i * span, span), span)])
        return c

    lax.fori_loop(0, devices // group, scatter_cameras, 0)
    sums = cacc[0:32] + cacc[32:64]

    zeros2 = jnp.zeros((2, cams), F32)
    spot = {}
    for r, (a, b) in enumerate(PAIRS):
        spot[a, b] = r
        spot[b, a] = r
    columns = [
        jnp.concatenate([sums[spot[a, b] : spot[a, b] + 1] for a in range(6)] + [zeros2], 0)
        for b in range(6)
    ]
    diagonal = DAMPING + jnp.concatenate(
        [sums[spot[a, a] : spot[a, a] + 1] for a in range(6)] + [zeros2], 0
    )
    keep = iota((8, slots), 0) < 6
    flag = jnp.logical_and(
        iota((8, slots), 0) == 6, jnp.bitwise_and(iota((8, slots), 1), 15) == 0
    )

    def total_of(x):
        return jnp.sum(jnp.sum(x, 0, keepdims=True), 1, keepdims=True)

    def exchange(rnd, values, scalar):
        txc[rnd] = to_rows(jnp.where(flag, scalar, values))
        send(2 + rnd, txc.at[rnd], rxc.at[rnd], 1)
        wait(2 + rnd, rxc.at[rnd], 1, recv_sem)
        raw = to_columns(rxc[rnd])
        return jnp.where(keep, raw, 0.0), total_of(jnp.where(flag, raw, 0.0))

    def to_slots(x):
        got = dot(split3(x), ohs)
        return got[0:8] + got[8:16] + got[16:24]

    def from_slots(x):
        got = dot_nt(split3(x), ohs)
        return got[0:8] + got[8:16] + got[16:24]

    def near(x):
        x = split2(x)
        got = dot(x, s_hi[...]) + dot(x, s_lo[...])
        return got[0:8] + got[8:16]

    def flow(x):
        x = split2(x)
        got = dot_nt(x, s_hi[...]) + dot_nt(x, s_lo[...])
        return got[0:8] + got[8:16]

    residual = -jnp.concatenate([sums[21:27], zeros2], 0)
    step = jnp.zeros((8, cams), F32)
    precond = residual / diagonal
    direction = incoming = rz = None
    for it in range(ITERS):
        arrived, new = exchange(2 * it, to_slots(precond), total_of(residual * precond))
        if it == 0:
            direction, incoming = precond, arrived
        else:
            beta = new / rz
            direction = precond + beta * direction
            incoming = arrived + beta * incoming
        rz = new
        around = near(incoming)
        local = (DAMPING + degree) * direction - around
        for b in range(6):
            local = local + columns[b] * direction[b : b + 1]
        energy = total_of(direction * (local - around)) + total_of(
            slot_degree * incoming * incoming
        )
        back, curve = exchange(2 * it + 1, flow(direction) - slot_degree * incoming, energy)
        image = local - from_slots(back)
        alpha = rz / curve
        step = step + alpha * direction
        residual = residual - alpha * image
        if it + 1 < ITERS:
            precond = residual / diagonal
    step_ref[...] = step[0:6]
    res_ref[...] = residual[0:6]
    wait(0, tx1, 8, send_sem)
    wait(1, tx2, 8, send_sem)
    for rnd in range(2 * ITERS):
        wait(2 + rnd, txc.at[rnd], 1, send_sem)


def per_device(nx, ny, cam_pose, points, uv, obs_cam, obs_pt, count, send_list, es, ew):
    devices = nx * ny
    cams = cam_pose.shape[1]
    width = math.gcd(points.shape[1], 2 * LANES)
    levels = points.shape[1] // width
    slots = devices * send_list.shape[-1]
    vmem = pltpu.VMEM
    rounds = 2 * ITERS
    return pl.pallas_call(
        functools.partial(kernel, nx, ny),
        out_shape=[jax.ShapeDtypeStruct((6, cams), F32)] * 2,
        in_specs=[pl.BlockSpec(memory_space=vmem)] * 9,
        out_specs=[pl.BlockSpec(memory_space=vmem)] * 2,
        scratch_shapes=[
            vmem((devices * 8, LANES), F32),
            vmem((devices * 8, LANES), F32),
            vmem((devices * 8, LANES), F32),
            vmem((devices * 8, LANES), F32),
            vmem((rounds, devices, LANES), F32),
            vmem((rounds, devices, LANES), F32),
            vmem((width, devices * LANES), BF16),
            vmem((cams, devices * LANES), BF16),
            vmem((devices * 8, LANES), F32),
            vmem((devices * 16, LANES), F32),
            vmem((levels * 24, LANES), F32),
            vmem((levels * 24, LANES), F32),
            vmem((levels * 24, LANES), F32),
            vmem((levels * 24, LANES), F32),
            vmem((devices * 16, LANES), F32),
            vmem((devices * 32, LANES), F32),
            vmem((64, cams), F32),
            vmem((slots, cams), BF16),
            vmem((slots, cams), BF16),
            pltpu.SemaphoreType.DMA((2 + rounds,)),
            pltpu.SemaphoreType.DMA((2 + rounds,)),
        ],
        compiler_params=pltpu.CompilerParams(collective_id=0, has_side_effects=True),
    )(cam_pose, points, uv, obs_cam, obs_pt, count, send_list.reshape(1, slots), es, ew)


def solution(mesh):
    both = ("gx", "gy")
    return jax.shard_map(
        functools.partial(per_device, mesh.shape["gx"], mesh.shape["gy"]),
        mesh=mesh,
        in_specs=(
            P(None, both),
            P(None, both),
            P(None, both, None, None),
            P(both, None, None),
            P(both, None, None),
            P(both, None),
            P(both, None, None),
            P(None, both),
            P(None, both),
        ),
        out_specs=(P(None, both), P(None, both)),
        check_vma=False,
    )
```

```python
import functools
import math

import jax
import jax.numpy as jnp
from jax import lax
from jax.experimental import pallas as pl
from jax.experimental.pallas import tpu as pltpu
from jax.sharding import PartitionSpec as P

ITERS = 2
DAMPING = 1.0
LANES = 128
MESH = pl.DeviceIdType.MESH
PAIRS = [(a, b) for a in range(6) for b in range(a, 6)]
F32 = jnp.float32
BF16 = jnp.bfloat16


def iota(shape, axis):
    return lax.broadcasted_iota(jnp.int32, shape, axis)


def head(x):
    return x.astype(BF16).astype(F32)


def split2(x):
    high = head(x)
    return jnp.concatenate([high, x - high], 0).astype(BF16)


def split3(x):
    high = head(x)
    rest = x - high
    middle = head(rest)
    return jnp.concatenate([high, middle, rest - middle], 0).astype(BF16)


def dot(a, b):
    return jnp.dot(a, b, preferred_element_type=F32)


def dot_nt(a, b):
    return lax.dot_general(a, b, (((1,), (1,)), ((), ())), preferred_element_type=F32)


def block_transpose(x):
    off = jnp.bitwise_and((iota((8, LANES), 1) >> 4) - iota((8, LANES), 0), 7)
    out = x
    for s in range(1, 8):
        moved = pltpu.roll(pltpu.roll(x, 8 - s, 0), 16 * s, 1)
        out = jnp.where(off == s, moved, out)
    return out


def to_rows(x):
    tiles = x.shape[1] // LANES
    return jnp.concatenate(
        [block_transpose(x[:, t * LANES : (t + 1) * LANES]) for t in range(tiles)], 0
    )


def to_columns(x):
    tiles = x.shape[0] // 8
    return jnp.concatenate([block_transpose(x[8 * t : 8 * t + 8]) for t in range(tiles)], 1)


def kernel(
    nx,
    ny,
    cam_hbm,
    pts_hbm,
    uv_hbm,
    oc_hbm,
    op_hbm,
    cnt_hbm,
    snd_hbm,
    es_hbm,
    ew_hbm,
    out_ref,
    cam_ref,
    pts_ref,
    uv_ref,
    oc_ref,
    op_ref,
    cnt_ref,
    snd_ref,
    es_ref,
    ew_ref,
    tx1,
    rx1,
    tx2,
    rx2,
    txc,
    rxc,
    ohp,
    ohc,
    xbuf,
    vbuf,
    acc0,
    acc1,
    tab0,
    tab1,
    gbuf,
    cbuf,
    cacc,
    s_hi,
    s_lo,
    send_sem,
    recv_sem,
    load_sem,
):
    held_refs = (cam_ref, oc_ref, uv_ref, pts_ref, op_ref, es_ref, ew_ref, snd_ref, cnt_ref)
    hbm = (cam_hbm, oc_hbm, uv_hbm, pts_hbm, op_hbm, es_hbm, ew_hbm, snd_hbm, cnt_hbm)
    devices = nx * ny
    cams = cam_ref.shape[1]
    width = math.gcd(pts_ref.shape[1], 2 * LANES)
    levels = pts_ref.shape[1] // width
    group = math.gcd(devices, 8)
    span = group * LANES
    me = lax.axis_index("gx") * ny + lax.axis_index("gy")

    barrier = pltpu.get_barrier_semaphore()

    def greet(i, c):
        peer = lax.rem(me + i, devices)
        pl.semaphore_signal(
            barrier, inc=1, device_id=(peer // ny, lax.rem(peer, ny)), device_id_type=MESH
        )
        return c

    lax.fori_loop(1, devices, greet, 0, unroll=min(devices - 1, 31))
    loads = [
        pltpu.make_async_copy(far, close, load_sem.at[k])
        for k, (far, close) in enumerate(zip(hbm, held_refs))
    ]
    for load in loads:
        load.start()
    for load in loads[0:3]:
        load.wait()

    def send(rnd, tx, rx, rows):
        def one(i, c):
            peer = lax.rem(me + i, devices)
            pltpu.make_async_remote_copy(
                src_ref=tx.at[pl.ds(peer * rows, rows)],
                dst_ref=rx.at[pl.ds(me * rows, rows)],
                send_sem=send_sem.at[rnd],
                recv_sem=recv_sem.at[rnd],
                device_id=(peer // ny, lax.rem(peer, ny)),
                device_id_type=MESH,
            ).start()
            return c

        lax.fori_loop(1, devices, one, 0, unroll=min(devices - 1, 31))
        rx[pl.ds(me * rows, rows)] = tx[pl.ds(me * rows, rows)]

    def wait(rnd, ref, rows, sem):
        part = ref.at[pl.ds(0, (devices - 1) * rows)]
        pltpu.make_async_copy(part, part, sem.at[rnd]).wait()

    pose = cam_ref[...]
    table = split3(
        jnp.concatenate([jnp.zeros((2, cams), F32), pose[1:4] / pose[0:1], pose[4:7]], 0)
    )
    row8 = iota((8, LANES), 0)

    def gather_poses(i, c):
        rows = [oc_ref[0, pl.ds(i * group + g, 1), :] for g in range(group)]
        onehot = (iota((cams, span), 0) == jnp.concatenate(rows, 1)).astype(F32).astype(BF16)
        ohc[:, pl.ds(pl.multiple_of(i * span, span), span)] = onehot
        got = dot(table, onehot)
        got = got[0:8] + got[8:16] + got[16:24]
        for g in range(group):
            d = i * group + g
            block = got[:, g * LANES : (g + 1) * LANES]
            block = jnp.where(row8 == 0, uv_ref[0, 0, pl.ds(d, 1), :], block)
            block = jnp.where(row8 == 1, uv_ref[1, 0, pl.ds(d, 1), :], block)
            tx1[pl.ds(pl.multiple_of(d * 8, 8), 8), :] = block
        return c

    lax.fori_loop(0, devices // group, gather_poses, 0)
    pl.semaphore_wait(barrier, devices - 1)
    send(0, tx1, rx1, 8)

    for load in loads[3:]:
        load.wait()

    def level_mask(i):
        rows = [op_ref[0, pl.ds(i * group + g, 1), :] for g in range(group)]
        row = jnp.concatenate(rows, 1)
        level = row // width
        return row - level * width, (iota((levels, span), 0) == level).astype(F32)

    positions = jnp.concatenate([pts_ref[...], jnp.zeros((5, levels * width), F32)], 0)
    positions = split3(
        jnp.concatenate([positions[:, k * width : (k + 1) * width] for k in range(levels)], 0)
    )
    part = levels * 8

    def gather_tracks(i, c):
        low, mask = level_mask(i)
        onehot = (iota((width, span), 0) == low).astype(F32).astype(BF16)
        ohp[:, pl.ds(pl.multiple_of(i * span, span), span)] = onehot
        got = dot(positions, onehot)
        got = got[0:part] + got[part : 2 * part] + got[2 * part : 3 * part]
        total = jnp.zeros((8, span), F32)
        for k in range(levels):
            total = total + got[k * 8 : k * 8 + 8] * mask[k : k + 1]
        for g in range(group):
            d = i * group + g
            xbuf[pl.ds(pl.multiple_of(d * 8, 8), 8), :] = total[:, g * LANES : (g + 1) * LANES]
        return c

    lax.fori_loop(0, devices // group, gather_tracks, 0)

    each = snd_ref.shape[1]
    slots = devices * each
    piece = 64

    def weigh(i, c):
        slot = iota((piece, cams), 0) + i * piece
        total = jnp.zeros((piece, cams), F32)
        for k in range(es_ref.shape[0]):
            total = total + jnp.where(slot == es_ref[k : k + 1, :], ew_ref[k : k + 1, :], 0.0)
        high = head(total)
        at = pl.ds(pl.multiple_of(i * piece, piece), piece)
        s_hi[at, :] = high.astype(BF16)
        s_lo[at, :] = (total - high).astype(BF16)
        return c

    lax.fori_loop(0, slots // piece, weigh, 0)
    listed = snd_ref[0].astype(F32)
    tiled = iota((devices, slots), 1) // each == iota((devices, slots), 0)
    tiled = tiled.astype(F32).astype(BF16)
    listed = dot(head(listed).astype(BF16), tiled) + dot(
        (listed - head(listed)).astype(BF16), tiled
    )
    own = lax.rem(iota((each, slots), 1), each) == iota((each, slots), 0)
    listed = jnp.sum(jnp.where(own, listed, 0.0), 0, keepdims=True)
    ohs = (iota((cams, slots), 0).astype(F32) == listed).astype(F32).astype(BF16)
    degree = jnp.sum(ew_ref[...], 0, keepdims=True)
    ones = jnp.ones((16, cams), F32).astype(BF16)
    slot_degree = (dot_nt(ones, s_hi[...]) + dot_nt(ones, s_lo[...]))[0:8]
    row_degree = to_rows(slot_degree)

    spread = jnp.where(
        iota((devices, devices), 0) == iota((devices, devices), 1), cnt_ref[...].astype(F32), 0.0
    )
    count = jnp.sum(spread, 1, keepdims=True)
    live = (iota((devices, LANES), 1).astype(F32) < count).astype(F32)

    vbuf[...] = jnp.zeros_like(vbuf)
    acc0[...] = jnp.zeros_like(acc0)
    acc1[...] = jnp.zeros_like(acc1)
    tab0[...] = jnp.zeros_like(tab0)
    tab1[...] = jnp.zeros_like(tab1)
    cbuf[...] = jnp.zeros_like(cbuf)
    cacc[...] = jnp.zeros_like(cacc)

    wait(0, rx1, 8, recv_sem)

    def pick(ref, r, stride):
        return ref[pl.ds(r, devices, stride=stride), :]

    mu, mv, q1, q2, q3, t0, t1, t2 = [pick(rx1, r, 8) for r in range(8)]
    x0, x1, x2 = [pick(xbuf, r, 8) for r in range(3)]
    norm = 1.0 / (1.0 + q1 * q1 + q2 * q2 + q3 * q3)
    rot = [
        1.0 + q1 * q1 - q2 * q2 - q3 * q3,
        2.0 * (q1 * q2 - q3),
        2.0 * (q1 * q3 + q2),
        2.0 * (q1 * q2 + q3),
        1.0 - q1 * q1 + q2 * q2 - q3 * q3,
        2.0 * (q2 * q3 - q1),
        2.0 * (q1 * q3 - q2),
        2.0 * (q2 * q3 + q1),
        1.0 - q1 * q1 - q2 * q2 + q3 * q3,
    ]
    rot = [r * norm for r in rot]
    pa = rot[0] * x0 + rot[1] * x1 + rot[2] * x2 + t0
    pb = rot[3] * x0 + rot[4] * x1 + rot[5] * x2 + t1
    pe = rot[6] * x0 + rot[7] * x1 + rot[8] * x2 + t2
    inv = 1.0 / pe
    u = pa * inv
    v = pb * inv
    scaled = inv * live
    ru = (u - mu) * live
    rv = (v - mv) * live
    ju = [scaled * (rot[k] - u * rot[6 + k]) for k in range(3)]
    jv = [scaled * (rot[3 + k] - v * rot[6 + k]) for k in range(3)]
    terms = [ju[k] * ju[l] + jv[k] * jv[l] for k in range(3) for l in range(k, 3)]
    terms = terms + [ju[k] * ru + jv[k] * rv for k in range(3)]
    for r in range(8):
        vbuf[pl.ds(r, devices, stride=16), :] = terms[r]
    vbuf[pl.ds(8, devices, stride=16), :] = head(terms[8])
    vbuf[pl.ds(9, devices, stride=16), :] = terms[8] - head(terms[8])

    def scatter_tracks(i, c):
        _, mask = level_mask(i)
        blocks = [
            vbuf[pl.ds(pl.multiple_of((i * group + g) * 16, 16), 16), :] for g in range(group)
        ]
        block = jnp.concatenate(blocks, 1)
        high = head(block[0:8])
        rows = jnp.concatenate([high, block[0:8] - high, block[8:16]], 0)
        left = jnp.concatenate([rows * mask[k : k + 1] for k in range(levels)], 0).astype(BF16)
        added = dot_nt(left, ohp[:, pl.ds(pl.multiple_of(i * span, span), span)])
        acc0[...] += added[:, 0:LANES]
        acc1[...] += added[:, LANES:]
        return c

    lax.fori_loop(0, devices // group, scatter_tracks, 0)

    for acc, tab in ((acc0, tab0), (acc1, tab1)):

        def take(r):
            return acc[pl.ds(r, levels, stride=24), :]

        def put(r, value):
            tab[pl.ds(r, levels, stride=24), :] = value

        sums = [take(r) + take(8 + r) for r in range(8)] + [take(16) + take(17)]
        h0, h1, h2, h3, h4, h5 = sums[0:6]
        h0, h3, h5 = h0 + DAMPING, h3 + DAMPING, h5 + DAMPING
        cof = [
            h3 * h5 - h4 * h4,
            h2 * h4 - h1 * h5,
            h1 * h4 - h2 * h3,
            h0 * h5 - h2 * h2,
            h1 * h2 - h0 * h4,
            h0 * h3 - h1 * h1,
        ]
        invdet = 1.0 / (h0 * cof[0] + h1 * cof[1] + h2 * cof[2])
        cof = [value * invdet for value in cof]
        g0, g1, g2 = sums[6:9]
        cof = cof + [
            cof[0] * g0 + cof[1] * g1 + cof[2] * g2,
            cof[1] * g0 + cof[3] * g1 + cof[4] * g2,
            cof[2] * g0 + cof[4] * g1 + cof[5] * g2,
        ]
        for r in range(8):
            put(r, head(cof[r]))
            put(8 + r, cof[r] - head(cof[r]))
        put(16, head(cof[8]))
        put(17, cof[8] - head(cof[8]))

    inverse = jnp.concatenate([tab0[...], tab1[...]], 1).astype(BF16)

    def gather_inverse(i, c):
        _, mask = level_mask(i)
        got = dot(inverse, ohp[:, pl.ds(pl.multiple_of(i * span, span), span)])
        total = jnp.zeros((24, span), F32)
        for k in range(levels):
            total = total + got[k * 24 : k * 24 + 24] * mask[k : k + 1]
        total = jnp.concatenate([total[0:8] + total[8:16], total[16:24]], 0)
        for g in range(group):
            at = pl.ds(pl.multiple_of((i * group + g) * 16, 16), 16)
            gbuf[at, :] = total[:, g * LANES : (g + 1) * LANES]
        return c

    lax.fori_loop(0, devices // group, gather_inverse, 0)

    n = [pick(gbuf, r, 16) for r in range(8)]
    n.append(pick(gbuf, 8, 16) + pick(gbuf, 9, 16))
    full = [[n[0], n[1], n[2]], [n[1], n[3], n[4]], [n[2], n[4], n[5]]]
    nu = [sum(full[k][l] * ju[l] for l in range(3)) for k in range(3)]
    nv = [sum(full[k][l] * jv[l] for l in range(3)) for k in range(3)]
    out = [
        live - sum(ju[k] * nu[k] for k in range(3)),
        -sum(ju[k] * nv[k] for k in range(3)),
        live - sum(jv[k] * nv[k] for k in range(3)),
        ru - sum(ju[k] * n[6 + k] for k in range(3)),
        rv - sum(jv[k] * n[6 + k] for k in range(3)),
        inv,
        u,
        v,
    ]
    for r in range(8):
        tx2[pl.ds(r, devices, stride=8), :] = out[r]
    send(1, tx2, rx2, 8)
    wait(1, rx2, 8, recv_sem)

    muu, muv, mvv, eu, ev, inv, u, v = [pick(rx2, r, 8) for r in range(8)]
    cu = [-u * v, 1.0 + u * u, -v, inv, None, -u * inv]
    cv = [-1.0 - v * v, u * v, u, None, inv, -v * inv]

    def combine(first, second):
        kept = [a * b for a, b in (first, second) if b is not None]
        return kept[0] if len(kept) == 1 else kept[0] + kept[1]

    wu = [combine((muu, cu[a]), (muv, cv[a])) for a in range(6)]
    wv = [combine((muv, cu[a]), (mvv, cv[a])) for a in range(6)]
    for r, (a, b) in enumerate(PAIRS):
        cbuf[pl.ds(r, devices, stride=32), :] = combine((wu[a], cu[b]), (wv[a], cv[b]))
    for a in range(6):
        cbuf[pl.ds(21 + a, devices, stride=32), :] = combine((eu, cu[a]), (ev, cv[a]))

    def scatter_cameras(i, c):
        blocks = [
            cbuf[pl.ds(pl.multiple_of((i * group + g) * 32, 32), 32), :] for g in range(group)
        ]
        left = split2(jnp.concatenate(blocks, 1))
        cacc[...] += dot_nt(left, ohc[:, pl.ds(pl.multiple_of(i * span, span), span)])
        return c

    lax.fori_loop(0, devices // group, scatter_cameras, 0)
    sums = cacc[0:32] + cacc[32:64]

    zeros2 = jnp.zeros((2, cams), F32)
    spot = {}
    for r, (a, b) in enumerate(PAIRS):
        spot[a, b] = r
        spot[b, a] = r
    columns = [
        jnp.concatenate([sums[spot[a, b] : spot[a, b] + 1] for a in range(6)] + [zeros2], 0)
        for b in range(6)
    ]
    diagonal = DAMPING + jnp.concatenate(
        [sums[spot[a, a] : spot[a, a] + 1] for a in range(6)] + [zeros2], 0
    )
    lane = iota((devices, LANES), 1)
    held = 6 * each

    def total_of(x):
        return jnp.sum(jnp.sum(x, 0, keepdims=True), 1, keepdims=True)

    def start(rnd, rows):
        txc[rnd] = rows
        send(2 + rnd, txc.at[rnd], rxc.at[rnd], 1)

    def finish(rnd):
        wait(2 + rnd, rxc.at[rnd], 1, recv_sem)
        return rxc[rnd]

    def to_slots(x):
        got = dot(split3(x), ohs)
        return got[0:8] + got[8:16] + got[16:24]

    def from_slots(x):
        got = dot_nt(split3(x), ohs)
        return got[0:8] + got[8:16] + got[16:24]

    def near(x):
        x = split2(x)
        got = dot(x, s_hi[...]) + dot(x, s_lo[...])
        return got[0:8] + got[8:16]

    def flow(x):
        x = split2(x)
        got = dot_nt(x, s_hi[...]) + dot_nt(x, s_lo[...])
        return got[0:8] + got[8:16]

    def block_product(x):
        total = (DAMPING + degree) * x
        for b in range(6):
            total = total + columns[b] * x[b : b + 1]
        return total

    residual = -jnp.concatenate([sums[21:27], zeros2], 0)
    inverse_diagonal = 1.0 / diagonal
    step = jnp.zeros((8, cams), F32)
    precond = residual * inverse_diagonal
    rows = to_rows(to_slots(precond))
    direction = image = curve = rz = None
    for it in range(ITERS):
        start(2 * it, rows)
        local = block_product(precond)
        flowing = to_rows(flow(precond))
        energy = total_of(precond * local)
        new = total_of(residual * precond)
        mixed = new if it == 0 else total_of(precond * image)
        arrived = finish(2 * it)
        weighed = row_degree * arrived
        energy = energy + total_of(arrived * (weighed - 2.0 * flowing))
        sent = flowing - weighed
        sent = jnp.where(lane == held + 1, new, sent)
        sent = jnp.where(lane == held + 2, mixed, sent)
        sent = jnp.where(lane == held, energy, sent)
        start(2 * it + 1, sent)
        local = local - near(to_columns(arrived))
        back = finish(2 * it + 1)
        added = jnp.sum(back, 0, keepdims=True)
        energy, new, mixed = [
            jnp.sum(jnp.where(lane[0:1] == held + k, added, 0.0), 1, keepdims=True)
            for k in range(3)
        ]
        fresh = local - from_slots(to_columns(jnp.where(lane < held, back, 0.0)))
        if it == 0:
            direction, image, curve = precond, fresh, energy
        else:
            beta = new / rz
            direction = precond + beta * direction
            image = fresh + beta * image
            curve = energy + beta * (2.0 * mixed + beta * curve)
        rz = new
        alpha = rz / curve
        if it + 1 < ITERS:
            rows = rows - alpha * to_rows(to_slots(image * inverse_diagonal))
        step = step + alpha * direction
        residual = residual - alpha * image
        precond = residual * inverse_diagonal
    out_ref[0] = step[0:6]
    out_ref[1] = residual[0:6]
    wait(0, tx1, 8, send_sem)
    wait(1, tx2, 8, send_sem)
    for rnd in range(2 * ITERS):
        wait(2 + rnd, txc.at[rnd], 1, send_sem)


def per_device(nx, ny, cam_pose, points, uv, obs_cam, obs_pt, count, send_list, es, ew):
    devices = nx * ny
    cams = cam_pose.shape[1]
    width = math.gcd(points.shape[1], 2 * LANES)
    levels = points.shape[1] // width
    slots = devices * send_list.shape[-1]
    turned = jnp.swapaxes(send_list, 1, 2)
    operands = (cam_pose, points, uv, obs_cam, obs_pt, count, turned, es, ew)
    vmem = pltpu.VMEM
    rounds = 2 * ITERS
    out = pl.pallas_call(
        functools.partial(kernel, nx, ny),
        out_shape=jax.ShapeDtypeStruct((2, 6, cams), F32),
        in_specs=[pl.BlockSpec(memory_space=pl.ANY)] * 9,
        out_specs=pl.BlockSpec(memory_space=vmem),
        scratch_shapes=[vmem(x.shape, x.dtype) for x in operands]
        + [
            vmem((devices * 8, LANES), F32),
            vmem((devices * 8, LANES), F32),
            vmem((devices * 8, LANES), F32),
            vmem((devices * 8, LANES), F32),
            vmem((rounds, devices, LANES), F32),
            vmem((rounds, devices, LANES), F32),
            vmem((width, devices * LANES), BF16),
            vmem((cams, devices * LANES), BF16),
            vmem((devices * 8, LANES), F32),
            vmem((devices * 16, LANES), F32),
            vmem((levels * 24, LANES), F32),
            vmem((levels * 24, LANES), F32),
            vmem((levels * 24, LANES), F32),
            vmem((levels * 24, LANES), F32),
            vmem((devices * 16, LANES), F32),
            vmem((devices * 32, LANES), F32),
            vmem((64, cams), F32),
            vmem((slots, cams), BF16),
            vmem((slots, cams), BF16),
            pltpu.SemaphoreType.DMA((2 + rounds,)),
            pltpu.SemaphoreType.DMA((2 + rounds,)),
            pltpu.SemaphoreType.DMA((len(operands),)),
        ],
        compiler_params=pltpu.CompilerParams(collective_id=0, has_side_effects=True),
    )(*operands)
    return out[0], out[1]


def solution(mesh):
    both = ("gx", "gy")
    return jax.shard_map(
        functools.partial(per_device, mesh.shape["gx"], mesh.shape["gy"]),
        mesh=mesh,
        in_specs=(
            P(None, both),
            P(None, both),
            P(None, both, None, None),
            P(both, None, None),
            P(both, None, None),
            P(both, None),
            P(both, None, None),
            P(None, both),
            P(None, both),
        ),
        out_specs=(P(None, both), P(None, both)),
        check_vma=False,
    )
```

```python
import functools
import math

import jax
import jax.numpy as jnp
from jax import lax
from jax.experimental import pallas as pl
from jax.experimental.pallas import tpu as pltpu
from jax.sharding import PartitionSpec as P

ITERS = 2
DAMPING = 1.0
LANES = 128
MESH = pl.DeviceIdType.MESH
PAIRS = [(a, b) for a in range(6) for b in range(a, 6)]
F32 = jnp.float32
BF16 = jnp.bfloat16


def iota(shape, axis):
    return lax.broadcasted_iota(jnp.int32, shape, axis)


def head(x):
    return x.astype(BF16).astype(F32)


def split2(x):
    high = head(x)
    return jnp.concatenate([high, x - high], 0).astype(BF16)


def split3(x):
    high = head(x)
    rest = x - high
    middle = head(rest)
    return jnp.concatenate([high, middle, rest - middle], 0).astype(BF16)


def dot(a, b):
    return jnp.dot(a, b, preferred_element_type=F32)


def dot_nt(a, b):
    return lax.dot_general(a, b, (((1,), (1,)), ((), ())), preferred_element_type=F32)


def block_transpose(x):
    off = jnp.bitwise_and((iota((8, LANES), 1) >> 4) - iota((8, LANES), 0), 7)
    out = x
    for s in range(1, 8):
        moved = pltpu.roll(pltpu.roll(x, 8 - s, 0), 16 * s, 1)
        out = jnp.where(off == s, moved, out)
    return out


def to_rows(x):
    tiles = x.shape[1] // LANES
    return jnp.concatenate(
        [block_transpose(x[:, t * LANES : (t + 1) * LANES]) for t in range(tiles)], 0
    )


def to_columns(x):
    tiles = x.shape[0] // 8
    return jnp.concatenate([block_transpose(x[8 * t : 8 * t + 8]) for t in range(tiles)], 1)


def kernel(
    nx,
    ny,
    cam_hbm,
    pts_hbm,
    uv_hbm,
    oc_hbm,
    op_hbm,
    cnt_hbm,
    snd_hbm,
    es_hbm,
    ew_hbm,
    out_ref,
    cam_ref,
    pts_ref,
    uv_ref,
    oc_ref,
    op_ref,
    cnt_ref,
    snd_ref,
    es_ref,
    ew_ref,
    tx1,
    rx1,
    tx2,
    rx2,
    txc,
    rxc,
    ohp,
    ohc,
    xbuf,
    vbuf,
    acc0,
    acc1,
    tab0,
    tab1,
    gbuf,
    kept,
    cbuf,
    cacc,
    s_hi,
    s_lo,
    send_sem,
    recv_sem,
    load_sem,
):
    held_refs = (cam_ref, oc_ref, uv_ref, pts_ref, op_ref, es_ref, ew_ref, snd_ref, cnt_ref)
    hbm = (cam_hbm, oc_hbm, uv_hbm, pts_hbm, op_hbm, es_hbm, ew_hbm, snd_hbm, cnt_hbm)
    devices = nx * ny
    cams = cam_ref.shape[1]
    width = math.gcd(pts_ref.shape[1], 2 * LANES)
    levels = pts_ref.shape[1] // width
    group = math.gcd(devices, 8)
    span = group * LANES
    me = lax.axis_index("gx") * ny + lax.axis_index("gy")

    barrier = pltpu.get_barrier_semaphore()

    def greet(i, c):
        peer = lax.rem(me + i, devices)
        pl.semaphore_signal(
            barrier, inc=1, device_id=(peer // ny, lax.rem(peer, ny)), device_id_type=MESH
        )
        return c

    lax.fori_loop(1, devices, greet, 0, unroll=min(devices - 1, 31))
    loads = [
        pltpu.make_async_copy(far, close, load_sem.at[k])
        for k, (far, close) in enumerate(zip(hbm, held_refs))
    ]
    for load in loads:
        load.start()
    for load in loads[0:3]:
        load.wait()

    def send_one(rnd, tx, rx, rows, peer):
        pltpu.make_async_remote_copy(
            src_ref=tx.at[pl.ds(peer * rows, rows)],
            dst_ref=rx.at[pl.ds(me * rows, rows)],
            send_sem=send_sem.at[rnd],
            recv_sem=recv_sem.at[rnd],
            device_id=(peer // ny, lax.rem(peer, ny)),
            device_id_type=MESH,
        ).start()

    def send(rnd, tx, rx, rows):
        def one(i, c):
            send_one(rnd, tx, rx, rows, lax.rem(me + i, devices))
            return c

        lax.fori_loop(1, devices, one, 0, unroll=min(devices - 1, 31))
        rx[pl.ds(me * rows, rows)] = tx[pl.ds(me * rows, rows)]

    def wait(rnd, ref, rows, sem):
        part = ref.at[pl.ds(0, (devices - 1) * rows)]
        pltpu.make_async_copy(part, part, sem.at[rnd]).wait()

    pose = cam_ref[...]
    table = split3(
        jnp.concatenate([jnp.zeros((2, cams), F32), pose[1:4] / pose[0:1], pose[4:7]], 0)
    )
    row8 = iota((8, LANES), 0)

    def gather_poses(i, c):
        rows = [oc_ref[0, pl.ds(i * group + g, 1), :] for g in range(group)]
        onehot = (iota((cams, span), 0) == jnp.concatenate(rows, 1)).astype(F32).astype(BF16)
        ohc[:, pl.ds(pl.multiple_of(i * span, span), span)] = onehot
        got = dot(table, onehot)
        got = got[0:8] + got[8:16] + got[16:24]
        for g in range(group):
            d = i * group + g
            block = got[:, g * LANES : (g + 1) * LANES]
            block = jnp.where(row8 == 0, uv_ref[0, 0, pl.ds(d, 1), :], block)
            block = jnp.where(row8 == 1, uv_ref[1, 0, pl.ds(d, 1), :], block)
            tx1[pl.ds(pl.multiple_of(d * 8, 8), 8), :] = block
        return c

    lax.fori_loop(0, devices // group, gather_poses, 0)
    pl.semaphore_wait(barrier, devices - 1)
    send(0, tx1, rx1, 8)

    for load in loads[3:]:
        load.wait()

    def level_mask(i):
        rows = [op_ref[0, pl.ds(i * group + g, 1), :] for g in range(group)]
        row = jnp.concatenate(rows, 1)
        level = row // width
        return row - level * width, (iota((levels, span), 0) == level).astype(F32)

    positions = jnp.concatenate([pts_ref[...], jnp.zeros((5, levels * width), F32)], 0)
    positions = split3(
        jnp.concatenate([positions[:, k * width : (k + 1) * width] for k in range(levels)], 0)
    )
    part = levels * 8

    def gather_tracks(i, c):
        low, mask = level_mask(i)
        onehot = (iota((width, span), 0) == low).astype(F32).astype(BF16)
        ohp[:, pl.ds(pl.multiple_of(i * span, span), span)] = onehot
        got = dot(positions, onehot)
        got = got[0:part] + got[part : 2 * part] + got[2 * part : 3 * part]
        total = jnp.zeros((8, span), F32)
        for k in range(levels):
            total = total + got[k * 8 : k * 8 + 8] * mask[k : k + 1]
        for g in range(group):
            d = i * group + g
            xbuf[pl.ds(pl.multiple_of(d * 8, 8), 8), :] = total[:, g * LANES : (g + 1) * LANES]
        return c

    lax.fori_loop(0, devices // group, gather_tracks, 0)

    each = snd_ref.shape[1]
    slots = devices * each
    piece = 64

    def weigh(i, c):
        slot = iota((piece, cams), 0) + i * piece
        total = jnp.zeros((piece, cams), F32)
        for k in range(es_ref.shape[0]):
            total = total + jnp.where(slot == es_ref[k : k + 1, :], ew_ref[k : k + 1, :], 0.0)
        high = head(total)
        at = pl.ds(pl.multiple_of(i * piece, piece), piece)
        s_hi[at, :] = high.astype(BF16)
        s_lo[at, :] = (total - high).astype(BF16)
        return c

    lax.fori_loop(0, slots // piece, weigh, 0)
    listed = snd_ref[0].astype(F32)
    tiled = iota((devices, slots), 1) // each == iota((devices, slots), 0)
    tiled = tiled.astype(F32).astype(BF16)
    listed = dot(head(listed).astype(BF16), tiled) + dot(
        (listed - head(listed)).astype(BF16), tiled
    )
    own = lax.rem(iota((each, slots), 1), each) == iota((each, slots), 0)
    listed = jnp.sum(jnp.where(own, listed, 0.0), 0, keepdims=True)
    ohs = (iota((cams, slots), 0).astype(F32) == listed).astype(F32).astype(BF16)
    degree = jnp.sum(ew_ref[...], 0, keepdims=True)
    ones = jnp.ones((16, cams), F32).astype(BF16)
    slot_degree = (dot_nt(ones, s_hi[...]) + dot_nt(ones, s_lo[...]))[0:8]
    row_degree = to_rows(slot_degree)

    spread = jnp.where(
        iota((devices, devices), 0) == iota((devices, devices), 1), cnt_ref[...].astype(F32), 0.0
    )
    count = jnp.sum(spread, 1, keepdims=True)
    live = (iota((devices, LANES), 1).astype(F32) < count).astype(F32)

    vbuf[...] = jnp.zeros_like(vbuf)
    acc0[...] = jnp.zeros_like(acc0)
    acc1[...] = jnp.zeros_like(acc1)
    tab0[...] = jnp.zeros_like(tab0)
    tab1[...] = jnp.zeros_like(tab1)
    cbuf[...] = jnp.zeros_like(cbuf)
    cacc[...] = jnp.zeros_like(cacc)

    wait(0, rx1, 8, recv_sem)

    def pick(ref, r, stride):
        return ref[pl.ds(r, devices, stride=stride), :]

    mu, mv, q1, q2, q3, t0, t1, t2 = [pick(rx1, r, 8) for r in range(8)]
    x0, x1, x2 = [pick(xbuf, r, 8) for r in range(3)]
    norm = 1.0 / (1.0 + q1 * q1 + q2 * q2 + q3 * q3)
    rot = [
        1.0 + q1 * q1 - q2 * q2 - q3 * q3,
        2.0 * (q1 * q2 - q3),
        2.0 * (q1 * q3 + q2),
        2.0 * (q1 * q2 + q3),
        1.0 - q1 * q1 + q2 * q2 - q3 * q3,
        2.0 * (q2 * q3 - q1),
        2.0 * (q1 * q3 - q2),
        2.0 * (q2 * q3 + q1),
        1.0 - q1 * q1 - q2 * q2 + q3 * q3,
    ]
    rot = [r * norm for r in rot]
    pa = rot[0] * x0 + rot[1] * x1 + rot[2] * x2 + t0
    pb = rot[3] * x0 + rot[4] * x1 + rot[5] * x2 + t1
    pe = rot[6] * x0 + rot[7] * x1 + rot[8] * x2 + t2
    inv = 1.0 / pe
    u = pa * inv
    v = pb * inv
    scaled = inv * live
    ru = (u - mu) * live
    rv = (v - mv) * live
    ju = [scaled * (rot[k] - u * rot[6 + k]) for k in range(3)]
    jv = [scaled * (rot[3 + k] - v * rot[6 + k]) for k in range(3)]
    terms = [ju[k] * ju[l] + jv[k] * jv[l] for k in range(3) for l in range(k, 3)]
    terms = terms + [ju[k] * ru + jv[k] * rv for k in range(3)]
    for r in range(8):
        vbuf[pl.ds(r, devices, stride=16), :] = terms[r]
    vbuf[pl.ds(8, devices, stride=16), :] = head(terms[8])
    vbuf[pl.ds(9, devices, stride=16), :] = terms[8] - head(terms[8])

    def scatter_tracks(i, c):
        _, mask = level_mask(i)
        blocks = [
            vbuf[pl.ds(pl.multiple_of((i * group + g) * 16, 16), 16), :] for g in range(group)
        ]
        block = jnp.concatenate(blocks, 1)
        high = head(block[0:8])
        rows = jnp.concatenate([high, block[0:8] - high, block[8:16]], 0)
        left = jnp.concatenate([rows * mask[k : k + 1] for k in range(levels)], 0).astype(BF16)
        added = dot_nt(left, ohp[:, pl.ds(pl.multiple_of(i * span, span), span)])
        acc0[...] += added[:, 0:LANES]
        acc1[...] += added[:, LANES:]
        return c

    lax.fori_loop(0, devices // group, scatter_tracks, 0)

    for acc, tab in ((acc0, tab0), (acc1, tab1)):

        def take(r):
            return acc[pl.ds(r, levels, stride=24), :]

        def put(r, value):
            tab[pl.ds(r, levels, stride=24), :] = value

        sums = [take(r) + take(8 + r) for r in range(8)] + [take(16) + take(17)]
        h0, h1, h2, h3, h4, h5 = sums[0:6]
        h0, h3, h5 = h0 + DAMPING, h3 + DAMPING, h5 + DAMPING
        cof = [
            h3 * h5 - h4 * h4,
            h2 * h4 - h1 * h5,
            h1 * h4 - h2 * h3,
            h0 * h5 - h2 * h2,
            h1 * h2 - h0 * h4,
            h0 * h3 - h1 * h1,
        ]
        invdet = 1.0 / (h0 * cof[0] + h1 * cof[1] + h2 * cof[2])
        cof = [value * invdet for value in cof]
        g0, g1, g2 = sums[6:9]
        cof = cof + [
            cof[0] * g0 + cof[1] * g1 + cof[2] * g2,
            cof[1] * g0 + cof[3] * g1 + cof[4] * g2,
            cof[2] * g0 + cof[4] * g1 + cof[5] * g2,
        ]
        for r in range(8):
            put(r, head(cof[r]))
            put(8 + r, cof[r] - head(cof[r]))
        put(16, head(cof[8]))
        put(17, cof[8] - head(cof[8]))

    inverse = jnp.concatenate([tab0[...], tab1[...]], 1).astype(BF16)

    for r, value in enumerate(ju + jv + [ru, rv, inv, u, v, live]):
        kept[r] = value

    def give_back(step_index, c):
        i = lax.rem(me // group + 1 + step_index, devices // group)
        _, mask = level_mask(i)
        got = dot(inverse, ohp[:, pl.ds(pl.multiple_of(i * span, span), span)])
        total = jnp.zeros((24, span), F32)
        for k in range(levels):
            total = total + got[k * 24 : k * 24 + 24] * mask[k : k + 1]
        total = jnp.concatenate([total[0:8] + total[8:16], total[16:24]], 0)
        for g in range(group):
            gbuf[g * 16 : g * 16 + 16, :] = total[:, g * LANES : (g + 1) * LANES]
        n = [gbuf[pl.ds(r, group, stride=16), :] for r in range(10)]
        n[8] = n[8] + n[9]
        old = [kept[r, pl.ds(pl.multiple_of(i * group, group), group), :] for r in range(12)]
        ju, jv = old[0:3], old[3:6]
        ru, rv, inv, u, v, live = old[6:12]
        full = [[n[0], n[1], n[2]], [n[1], n[3], n[4]], [n[2], n[4], n[5]]]
        nu = [sum(full[k][l] * ju[l] for l in range(3)) for k in range(3)]
        nv = [sum(full[k][l] * jv[l] for l in range(3)) for k in range(3)]
        out = [
            live - sum(ju[k] * nu[k] for k in range(3)),
            -sum(ju[k] * nv[k] for k in range(3)),
            live - sum(jv[k] * nv[k] for k in range(3)),
            ru - sum(ju[k] * n[6 + k] for k in range(3)),
            rv - sum(jv[k] * n[6 + k] for k in range(3)),
            inv,
            u,
            v,
        ]
        for r in range(8):
            tx2[pl.ds(i * group * 8 + r, group, stride=8), :] = out[r]
        for g in range(group):
            peer = i * group + g

            @pl.when(peer != me)
            def _():
                send_one(1, tx2, rx2, 8, peer)

        return c

    lax.fori_loop(0, devices // group, give_back, 0)
    rx2[pl.ds(me * 8, 8)] = tx2[pl.ds(me * 8, 8)]
    wait(1, rx2, 8, recv_sem)

    muu, muv, mvv, eu, ev, inv, u, v = [pick(rx2, r, 8) for r in range(8)]
    cu = [-u * v, 1.0 + u * u, -v, inv, None, -u * inv]
    cv = [-1.0 - v * v, u * v, u, None, inv, -v * inv]

    def combine(first, second):
        terms = [a * b for a, b in (first, second) if b is not None]
        return terms[0] if len(terms) == 1 else terms[0] + terms[1]

    wu = [combine((muu, cu[a]), (muv, cv[a])) for a in range(6)]
    wv = [combine((muv, cu[a]), (mvv, cv[a])) for a in range(6)]
    for r, (a, b) in enumerate(PAIRS):
        cbuf[pl.ds(r, devices, stride=32), :] = combine((wu[a], cu[b]), (wv[a], cv[b]))
    for a in range(6):
        cbuf[pl.ds(21 + a, devices, stride=32), :] = combine((eu, cu[a]), (ev, cv[a]))

    def scatter_cameras(i, c):
        blocks = [
            cbuf[pl.ds(pl.multiple_of((i * group + g) * 32, 32), 32), :] for g in range(group)
        ]
        left = split2(jnp.concatenate(blocks, 1))
        cacc[...] += dot_nt(left, ohc[:, pl.ds(pl.multiple_of(i * span, span), span)])
        return c

    lax.fori_loop(0, devices // group, scatter_cameras, 0)
    sums = cacc[0:32] + cacc[32:64]

    zeros2 = jnp.zeros((2, cams), F32)
    spot = {}
    for r, (a, b) in enumerate(PAIRS):
        spot[a, b] = r
        spot[b, a] = r
    columns = [
        jnp.concatenate([sums[spot[a, b] : spot[a, b] + 1] for a in range(6)] + [zeros2], 0)
        for b in range(6)
    ]
    diagonal = DAMPING + jnp.concatenate(
        [sums[spot[a, a] : spot[a, a] + 1] for a in range(6)] + [zeros2], 0
    )
    lane = iota((devices, LANES), 1)
    held = 6 * each

    def total_of(x):
        return jnp.sum(jnp.sum(x, 0, keepdims=True), 1, keepdims=True)

    def start(rnd, rows):
        txc[rnd] = rows
        send(2 + rnd, txc.at[rnd], rxc.at[rnd], 1)

    def finish(rnd):
        wait(2 + rnd, rxc.at[rnd], 1, recv_sem)
        return rxc[rnd]

    def to_slots(x):
        got = dot(split3(x), ohs)
        return got[0:8] + got[8:16] + got[16:24]

    def from_slots(x):
        got = dot_nt(split3(x), ohs)
        return got[0:8] + got[8:16] + got[16:24]

    def near(x):
        x = split2(x)
        got = dot(x, s_hi[...]) + dot(x, s_lo[...])
        return got[0:8] + got[8:16]

    def flow(x):
        x = split2(x)
        got = dot_nt(x, s_hi[...]) + dot_nt(x, s_lo[...])
        return got[0:8] + got[8:16]

    def block_product(x):
        total = (DAMPING + degree) * x
        for b in range(6):
            total = total + columns[b] * x[b : b + 1]
        return total

    residual = -jnp.concatenate([sums[21:27], zeros2], 0)
    inverse_diagonal = 1.0 / diagonal
    step = jnp.zeros((8, cams), F32)
    precond = residual * inverse_diagonal
    rows = to_rows(to_slots(precond))
    direction = image = curve = rz = None
    for it in range(ITERS):
        start(2 * it, rows)
        local = block_product(precond)
        flowing = to_rows(flow(precond))
        energy = total_of(precond * local)
        new = total_of(residual * precond)
        mixed = new if it == 0 else total_of(precond * image)
        arrived = finish(2 * it)
        weighed = row_degree * arrived
        energy = energy + total_of(arrived * (weighed - 2.0 * flowing))
        sent = flowing - weighed
        sent = jnp.where(lane == held + 1, new, sent)
        sent = jnp.where(lane == held + 2, mixed, sent)
        sent = jnp.where(lane == held, energy, sent)
        start(2 * it + 1, sent)
        local = local - near(to_columns(arrived))
        back = finish(2 * it + 1)
        added = jnp.sum(back, 0, keepdims=True)
        energy, new, mixed = [
            jnp.sum(jnp.where(lane[0:1] == held + k, added, 0.0), 1, keepdims=True)
            for k in range(3)
        ]
        fresh = local - from_slots(to_columns(jnp.where(lane < held, back, 0.0)))
        if it == 0:
            direction, image, curve = precond, fresh, energy
        else:
            beta = new / rz
            direction = precond + beta * direction
            image = fresh + beta * image
            curve = energy + beta * (2.0 * mixed + beta * curve)
        rz = new
        alpha = rz / curve
        if it + 1 < ITERS:
            rows = rows - alpha * to_rows(to_slots(image * inverse_diagonal))
        step = step + alpha * direction
        residual = residual - alpha * image
        precond = residual * inverse_diagonal
    out_ref[0] = step[0:6]
    out_ref[1] = residual[0:6]
    wait(0, tx1, 8, send_sem)
    wait(1, tx2, 8, send_sem)
    for rnd in range(2 * ITERS):
        wait(2 + rnd, txc.at[rnd], 1, send_sem)


def per_device(nx, ny, cam_pose, points, uv, obs_cam, obs_pt, count, send_list, es, ew):
    devices = nx * ny
    cams = cam_pose.shape[1]
    width = math.gcd(points.shape[1], 2 * LANES)
    levels = points.shape[1] // width
    slots = devices * send_list.shape[-1]
    turned = jnp.swapaxes(send_list, 1, 2)
    operands = (cam_pose, points, uv, obs_cam, obs_pt, count, turned, es, ew)
    vmem = pltpu.VMEM
    rounds = 2 * ITERS
    out = pl.pallas_call(
        functools.partial(kernel, nx, ny),
        out_shape=jax.ShapeDtypeStruct((2, 6, cams), F32),
        in_specs=[pl.BlockSpec(memory_space=pl.ANY)] * 9,
        out_specs=pl.BlockSpec(memory_space=vmem),
        scratch_shapes=[vmem(x.shape, x.dtype) for x in operands]
        + [
            vmem((devices * 8, LANES), F32),
            vmem((devices * 8, LANES), F32),
            vmem((devices * 8, LANES), F32),
            vmem((devices * 8, LANES), F32),
            vmem((rounds, devices, LANES), F32),
            vmem((rounds, devices, LANES), F32),
            vmem((width, devices * LANES), BF16),
            vmem((cams, devices * LANES), BF16),
            vmem((devices * 8, LANES), F32),
            vmem((devices * 16, LANES), F32),
            vmem((levels * 24, LANES), F32),
            vmem((levels * 24, LANES), F32),
            vmem((levels * 24, LANES), F32),
            vmem((levels * 24, LANES), F32),
            vmem((math.gcd(devices, 8) * 16, LANES), F32),
            vmem((12, devices, LANES), F32),
            vmem((devices * 32, LANES), F32),
            vmem((64, cams), F32),
            vmem((slots, cams), BF16),
            vmem((slots, cams), BF16),
            pltpu.SemaphoreType.DMA((2 + rounds,)),
            pltpu.SemaphoreType.DMA((2 + rounds,)),
            pltpu.SemaphoreType.DMA((len(operands),)),
        ],
        compiler_params=pltpu.CompilerParams(collective_id=0, has_side_effects=True),
    )(*operands)
    return out[0], out[1]


def solution(mesh):
    both = ("gx", "gy")
    return jax.shard_map(
        functools.partial(per_device, mesh.shape["gx"], mesh.shape["gy"]),
        mesh=mesh,
        in_specs=(
            P(None, both),
            P(None, both),
            P(None, both, None, None),
            P(both, None, None),
            P(both, None, None),
            P(both, None),
            P(both, None, None),
            P(None, both),
            P(None, both),
        ),
        out_specs=(P(None, both), P(None, both)),
        check_vma=False,
    )
```
